32 devices in a mesh: seg: 4 (over y, x), sec: 8 (over z, core).
Axes of the slice: x: 2, y: 2, z: 4, core: 2. Of those that a mesh axis runs over, the one named last changes fastest.
Arguments:
- left_env: bfloat16 [4, 8, 13, 512, 512], P('seg', 'sec'), may hold values from -0.25 to 0.25
- right_env: bfloat16 [4, 8, 13, 512, 512], P('seg', 'sec'), may hold values from -0.25 to 0.25
- left_block: bfloat16 [4, 8, 512, 512], P('seg', 'sec'), may hold values from -8 to 8
- right_block: bfloat16 [4, 8, 512, 512], P('seg', 'sec'), may hold values from -0.25 to 0.25
- inv_sv: bfloat16 [4, 8, 512], P('seg', 'sec'), may hold values from 0.5 to 2
- precond: float32 [4, 8, 512, 512], P('seg', 'sec'), may hold values from 1 to 4
- sector_dims: int32 [4, 8, 2], P('seg', 'sec'), may hold values from 128 to 512, as said below
- channel_charge: int32 [13], replicated, may hold values from -1 to 1
Outputs:
- next_vector: bfloat16 [4, 8, 512, 512], P('seg', 'sec')
- last_image: float32 [4, 8, 512, 512], P('seg', 'sec')
- projected: float32 [4, 4, 4], P('seg')
The draws below stay inside these ranges and needn't reach their ends.
Inputs may be any that keep to these rules, and one draw needn't show every extreme that they name: `sector_dims`: in every segment some sector has left bond dimension 512 and some sector has right bond dimension 512.
All inputs are finite; a program needn't handle non-finite values.
Results may differ from the reference program's by a relative error of at most 0.024.
Values may be sent and summed in bfloat16 or wider, within the bound.
A program may use at most 64 MiB of HBM per device.

```python
import math
import jax
import jax.numpy as jnp
from jax import lax

M = 512
W = 13
MATVECS = 4
SEGS = 4
SECTORS = 8


def draw_sector_dims(key, part):
    first_key, second_key = jax.random.split(jax.random.fold_in(key, 7))
    dims = jax.random.randint(first_key, (SEGS, SECTORS, 2), M // 4, M + 1)
    picked = jax.random.randint(second_key, (SEGS, 2), 0, SECTORS)
    hit = jnp.arange(SECTORS)[None, :, None] == picked[:, None, :]
    return jnp.where(hit, M, dims).astype(jnp.int32)


def draw_left_block(key, part):
    inner_key = jax.random.fold_in(key, 11)
    position = jnp.arange(SECTORS, dtype=jnp.float32) / max(SECTORS - 1, 1)
    factor = jnp.exp(jnp.log(0.4) + position * jnp.log(5.0))
    values = jax.random.normal(inner_key, (SEGS, SECTORS, M, M), jnp.float32)
    return jnp.clip(values * factor[None, :, None, None], -8.0, 8.0).astype(jnp.bfloat16)


def plant(drawn, stream_key, low, high):
    longest = drawn.shape.index(max(drawn.shape))
    spots = []
    for shift in (0, 1):
        where = [jax.random.randint(jax.random.fold_in(stream_key, axis), (), 0, length) for axis, length in enumerate(drawn.shape)]
        where[longest] = (where[longest] + shift) % drawn.shape[longest]
        spots.append(tuple(where))
    return drawn.at[spots[0]].set(low).at[spots[1]].set(high)


def steps_of(stream_key, shape, cuts, low, largest):
    def one(axis_at, shards_of):
        steps = jax.random.uniform(jax.random.fold_in(jax.random.fold_in(stream_key, 6), axis_at), (shards_of,), jnp.float32, low / len(cuts), largest / len(cuts))
        return jnp.repeat(jnp.exp(steps), shape[axis_at] // shards_of).reshape((-1,) + (1,) * (len(shape) - axis_at - 1))

    gain = one(*cuts[0])
    for cut in cuts[1:]:
        gain = gain * one(*cut)
    return gain


def gaussian(stream_key, shape, width, bound, cuts=(), kind=jnp.bfloat16):
    values = width * jax.random.normal(stream_key, shape, jnp.float32)
    if cuts:
        values = values * steps_of(stream_key, shape, cuts, -0.22, 0.18)
    return jnp.clip(values, -bound, bound).astype(kind)


def setup_inputs(seed: int = 0) -> dict:
    splits = jax.random.split(jax.random.key(seed), 9)
    return {
        "left_env": gaussian(splits[0], (SEGS, SECTORS, W, M, M), M ** -0.5, 0.25, ((0, 4), (1, 8))),
        "right_env": gaussian(splits[1], (SEGS, SECTORS, W, M, M), M ** -0.5, 0.25, ((0, 4), (1, 8))),
        "left_block": draw_left_block(jax.random.fold_in(splits[8], 71), 0),
        "right_block": gaussian(splits[3], (SEGS, SECTORS, M, M), M ** -0.5, 0.25, ((0, 4), (1, 8))),
        "inv_sv": jnp.clip(jnp.exp(math.log(2.0) - 1.3862944 * jax.random.uniform(splits[4], (SEGS, SECTORS, M), jnp.float32) ** steps_of(splits[4], (SEGS, SECTORS, M), ((0, 4), (1, 8)), -0.2, 0.2)), 0.5, 2.0).astype(jnp.bfloat16),
        "precond": jnp.clip(jnp.exp(math.log(4.0) - 1.3862944 * jax.random.uniform(splits[5], (SEGS, SECTORS, M, M), jnp.float32) ** steps_of(splits[5], (SEGS, SECTORS, M, M), ((0, 4), (1, 8)), -0.2, 0.2)), 1.0, 4.0),
        "sector_dims": draw_sector_dims(jax.random.fold_in(splits[8], 71), 0),
        "channel_charge": plant(jax.random.randint(splits[7], (W,), -1, 2), jax.random.fold_in(splits[7], 1), -1, 1).astype(jnp.int32),
    }


def reference(left_env, right_env, left_block, right_block, inv_sv, precond, sector_dims, channel_charge):
    eps = 1e-06
    index = jnp.arange(M, dtype=jnp.int32)
    mask = ((index[None, None, :, None] < sector_dims[:, :, 0, None, None]) & (index[None, None, None, :] < sector_dims[:, :, 1, None, None])).astype(jnp.float32)
    count = SECTORS * M * M

    def inner(first, second):
        return lax.optimization_barrier(jnp.sum(first * second, axis=(1, 2, 3))) / count

    def expand(value):
        return value[:, None, None, None]
    neighbour_block = jnp.roll(right_block, -1, axis=0)
    neighbour_inv = jnp.roll(inv_sv, -1, axis=0)
    scaled = (left_block.astype(jnp.float32) * neighbour_inv.astype(jnp.float32)[:, :, None, :]).astype(jnp.bfloat16)
    guess = jnp.einsum('gsab,gsbc->gsac', scaled.astype(jnp.float32), neighbour_block.astype(jnp.float32)) * mask
    first = (guess * expand(lax.rsqrt(inner(guess, guess) + eps))).astype(jnp.bfloat16)
    select = (channel_charge[:, None] == jnp.array([-1, 0, 1], dtype=jnp.int32)[None, :]).astype(jnp.float32)
    left_flat = left_env.reshape(SEGS * SECTORS, W, M, M)
    right_flat = right_env.reshape(SEGS * SECTORS, W, M, M)

    def apply(vector):
        vector_flat = vector.reshape(SEGS * SECTORS, M, M)

        def single(pieces):
            left_one, right_one, vec_one = pieces
            left_x = jnp.einsum('wab,bc->wac', left_one.astype(jnp.float32), vec_one.astype(jnp.float32)).astype(jnp.bfloat16)
            terms = jnp.einsum('wac,wdc->wad', left_x.astype(jnp.float32), right_one.astype(jnp.float32))
            return jnp.stack([lax.optimization_barrier(jnp.sum(terms * select[:, q, None, None], axis=0)) for q in range(3)])
        grouped = lax.map(single, (left_flat, right_flat, vector_flat)).reshape(SEGS, SECTORS, 3, M, M)
        to_lower = grouped[:, :, 0]
        stay = grouped[:, :, 1]
        to_upper = grouped[:, :, 2]
        zero = jnp.zeros_like(stay[:, :1])
        from_lower = jnp.concatenate([zero, to_upper[:, :-1]], axis=1)
        from_upper = jnp.concatenate([to_lower[:, 1:], zero], axis=1)
        return (stay + from_lower + from_upper) * mask
    basis = [first]
    columns = []
    image = None
    for step in range(MATVECS):
        current = basis[step]
        image = apply(current)
        column = [inner(basis[j].astype(jnp.float32), image) for j in range(step + 1)]
        column = column + [jnp.zeros((SEGS,), jnp.float32) for j in range(MATVECS - step - 1)]
        columns.append(jnp.stack(column, axis=1))
        theta = column[step]
        resid = image - expand(theta) * current.astype(jnp.float32)
        correction = resid / precond
        projected_part = jnp.zeros_like(correction)
        for j in range(step + 1):
            weight = inner(basis[j].astype(jnp.float32), correction)
            projected_part = projected_part + expand(weight) * basis[j].astype(jnp.float32)
        remain = correction - projected_part
        basis.append((remain * expand(lax.rsqrt(inner(remain, remain) + eps))).astype(jnp.bfloat16))
    projected = jnp.stack(columns, axis=2)
    return (basis[-1], image, projected)
```

```python
import functools

import jax
import jax.numpy as jnp
from jax import lax
from jax.experimental import pallas as pl
from jax.experimental.pallas import tpu as pltpu
from jax.sharding import PartitionSpec as P

MATVECS = 4
EPS = 1e-06
ROWS = 128
COLS = 256
CHUNK = 32
BLOCK = 64
LEAD = 3
QUANTITIES = 4 * MATVECS + 4
MESH = pl.DeviceIdType.MESH


def fold(values):
    rows, columns = values.shape
    block = jnp.sum(values.reshape(rows // 8, 8, columns), axis=0)
    total = block[:, :128]
    for at in range(128, columns, 128):
        total = total + block[:, at : at + 128]
    return total


def spread(tile, values):
    rows, columns = values.shape
    parts = []
    for at in range(0, columns, 128):
        part = values[:, at : at + 128].reshape(rows // 8, 8, 128) * tile[None]
        parts.append(part.reshape(rows, 128))
    return jnp.concatenate(parts, axis=1)


def kernel(
    segs, secs,
    charge_ref, dims_ref, left_hbm, right_hbm, block_hbm, other_hbm, inv_ref, precond_hbm,
    next_ref, image_ref, projected_ref,
    left_ref, right_ref, turned_ref, lx_even, lx_odd, block_ref, precond_ref, nb_ref, ninv_ref, scaled_ref, pinv_ref, basis_ref,
    prefix_even, prefix_odd, part_ref, x_ref, image_half, lifted_half, stay_ref, up_out, low_out, up_in, low_in, y_ref, norm_ref, slots_ref, rows_ref,
    tile_ref, alpha_ref, inner_ref, coef_ref, proj_ref, order_ref,
    load_sem, guess_send, guess_recv, halo_send, halo_recv, sum_send, sum_recv,
):
    channels, width, _ = left_ref.shape
    tiles = width // ROWS
    halves = width // COLS
    pieces = tiles * halves
    count = secs * width * width
    f32, bf16 = jnp.float32, jnp.bfloat16
    seg, sec = lax.axis_index("seg"), lax.axis_index("sec")
    seg_before = lax.rem(seg + segs - 1, segs)
    seg_after = lax.rem(seg + 1, segs)

    load_left = pltpu.make_async_copy(left_hbm, left_ref, load_sem.at[0])
    load_right = pltpu.make_async_copy(right_hbm, right_ref, load_sem.at[1])
    load_block = pltpu.make_async_copy(block_hbm, block_ref, load_sem.at[2])
    load_precond = pltpu.make_async_copy(precond_hbm, precond_ref, load_sem.at[3])
    load_precond.start()
    load_block.start()
    load_right.start()
    load_left.start()

    barrier = pltpu.get_barrier_semaphore()
    pl.semaphore_signal(barrier, inc=1, device_id=(seg_before, sec), device_id_type=MESH)
    pl.semaphore_signal(barrier, inc=1, device_id=(seg_after, sec), device_id_type=MESH)
    for offset in range(1, secs):
        peer = lax.rem(sec + offset, secs)
        pl.semaphore_signal(barrier, inc=1, device_id=(seg, peer), device_id_type=MESH)
    pl.semaphore_wait(barrier, secs + 1)

    def remote(src, dst, send, recv, device):
        return pltpu.make_async_remote_copy(
            src_ref=src, dst_ref=dst, send_sem=send, recv_sem=recv,
            device_id=device, device_id_type=MESH,
        )

    send_inv = remote(
        inv_ref, ninv_ref, guess_send.at[0], guess_recv.at[0], (seg_before, sec)
    )
    send_block = [
        remote(
            other_hbm.at[:, pl.ds(h * COLS, COLS)], nb_ref.at[h],
            guess_send.at[1 + h], guess_recv.at[1 + h], (seg_before, sec),
        )
        for h in range(halves)
    ]
    send_inv.start()
    for copy in send_block:
        copy.start()

    keys = []
    for w in range(channels):
        q = charge_ref[w]
        keys.append(jnp.where(q == 1, 0, jnp.where(q == -1, 1, 2)))
    raising = jnp.int32(0)
    moving = jnp.int32(0)
    for w in range(channels):
        raising = raising + jnp.where(keys[w] == 0, 1, 0)
        moving = moving + jnp.where(keys[w] <= 1, 1, 0)
    places = []
    for w in range(channels):
        place = jnp.int32(0)
        for v in range(channels):
            if v < w:
                place = place + jnp.where(keys[v] <= keys[w], 1, 0)
            elif v > w:
                place = place + jnp.where(keys[v] < keys[w], 1, 0)
        places.append(place)
    for i in range(channels):
        who = jnp.int32(0)
        for w in range(channels):
            who = who + jnp.where(places[w] == i, w, 0)
        order_ref[i] = who

    def masked(values, start, left=0):
        row = start + lax.broadcasted_iota(jnp.int32, values.shape, 0)
        column = left + lax.broadcasted_iota(jnp.int32, values.shape, 1)
        inside = (row < dims_ref[0]) & (column < dims_ref[1])
        return jnp.where(inside, values, 0.0)

    rows_ref[...] = jnp.zeros_like(rows_ref)
    proj_ref[...] = jnp.zeros_like(proj_ref)
    alpha_ref[...] = jnp.zeros_like(alpha_ref)
    lx_refs, prefix_refs = (lx_even, lx_odd), (prefix_even, prefix_odd)
    for prefix in prefix_refs:
        prefix[0] = jnp.zeros((ROWS, COLS), f32)

    @pl.loop(0, width // CHUNK)
    def _(c):
        at = pl.ds(pl.multiple_of(c * CHUNK, CHUNK), CHUNK)
        for k in range(MATVECS):
            basis_ref[k, at, :] = jnp.zeros((CHUNK, width), bf16)

    @pl.when(sec == 0)
    def _():
        @pl.loop(0, MATVECS * pieces)
        def _(n):
            up_in[n] = jnp.zeros((ROWS, COLS), bf16)

    @pl.when(sec == secs - 1)
    def _():
        @pl.loop(0, MATVECS * pieces)
        def _(n):
            low_in[n] = jnp.zeros((ROWS, COLS), bf16)

    load_precond.wait()

    @pl.loop(0, width // CHUNK)
    def _(c):
        at = pl.ds(pl.multiple_of(c * CHUNK, CHUNK), CHUNK)
        pinv_ref[at, :] = masked(1.0 / precond_ref[at, :], c * CHUNK)

    send_inv.wait_recv()
    load_block.wait()
    scaled_ref[...] = (
        block_ref[...].astype(f32) * ninv_ref[...].astype(f32)
    ).astype(bf16)

    load_right.wait()

    @pl.loop(0, channels)
    def _(w):
        for at in range(0, width, 128):
            turned_ref[w, :, at : at + 128] = right_ref[w, at : at + 128, :].T

    load_left.wait()

    def sum_copies(r):
        own = slots_ref.at[r, sec]
        return [
            remote(
                own, own, sum_send.at[r], sum_recv.at[r],
                (seg, lax.rem(sec + offset, secs)),
            )
            for offset in range(1, secs)
        ]

    def up_copy(n):
        return remote(
            up_out.at[n], up_in.at[n], halo_send.at[0, n], halo_recv.at[0, n],
            (seg, lax.rem(sec + 1, secs)),
        )

    def low_copy(n):
        return remote(
            low_out.at[n], low_in.at[n], halo_send.at[1, n], halo_recv.at[1, n],
            (seg, lax.rem(sec + secs - 1, secs)),
        )

    def rows_of(t):
        start = t * ROWS
        return pl.ds(start if isinstance(t, int) else pl.multiple_of(start, ROWS), ROWS)

    waiting = []

    def flush():
        while waiting:
            waiting.pop()()

    def first_product(t, lx, vector, inner):
        for w in range(channels):
            if w == LEAD:
                flush()
            lx[w, :, inner] = jnp.dot(
                left_ref[w, rows_of(t), :], vector, preferred_element_type=f32
            ).astype(bf16)

    def second_product(lx, h, inner):
        across = pl.ds(h * COLS, COLS)
        prefix = prefix_refs[h % 2]
        for i in range(channels):
            if i == LEAD:
                flush()
            w = order_ref[i]
            term = jnp.dot(
                lx[w, :, inner], turned_ref[w, inner, across], preferred_element_type=f32
            )
            prefix[i + 1] = prefix[i] + term

    def parts(h):
        prefix = prefix_refs[h % 2]
        first = prefix[raising]
        second = prefix[moving]
        return first, second - first, prefix[channels] - second

    def send(n, t, h, up, low, stay):
        up_out[n] = up.astype(bf16)
        low_out[n] = low.astype(bf16)

        @pl.when(sec < secs - 1)
        def _():
            up_copy(n).start()

        @pl.when(sec > 0)
        def _():
            low_copy(n).start()

        stay_ref[rows_of(t), pl.ds(h * COLS, COLS)] = stay

    def partial_done(s, t, h):
        found = parts(h)
        p = t * halves + h
        if s > 0:
            found = [part_ref[j, p] + value for j, value in enumerate(found)]
        if s < halves - 1:
            for j, value in enumerate(found):
                part_ref[j, p] = value
        else:
            send(p, t, h, *found)

    def done(n, t, h):
        send(n, t, h, *parts(h))

    def start_from_guess():
        norm_ref[...] = jnp.zeros_like(norm_ref)
        for s in range(halves):
            inner = pl.ds(s * COLS, COLS)
            send_block[s].wait_recv()

            @pl.loop(0, tiles)
            def _(t):
                value = masked(
                    jnp.dot(scaled_ref[rows_of(t), :], nb_ref[s], preferred_element_type=f32),
                    t * ROWS, s * COLS,
                )
                x_ref[rows_of(t), inner] = value.astype(bf16)
                norm_ref[...] += fold(value * value)

            @pl.loop(0, tiles, step=2)
            def _(start):
                for lead in range(2):
                    t = start + lead
                    first_product(t, lx_refs[lead], x_ref[:, inner], inner)
                    for h in range(halves):
                        second_product(lx_refs[lead], h, inner)
                        waiting.append(functools.partial(partial_done, s, t, h))
                flush()

    def refresh(rows, across):
        remain = spread(coef_ref[0], image_ref[rows, across])
        remain = remain - spread(coef_ref[1], x_ref[rows, across].astype(f32))
        remain = remain * pinv_ref[rows, across]
        for j in range(MATVECS):
            remain = remain - spread(coef_ref[2 + j], basis_ref[j, rows, across].astype(f32))
        return remain

    def continue_from(k):
        norm = jnp.zeros((8, 128), f32)
        for h in range(halves):
            across = pl.ds(h * COLS, COLS)
            for c in range(width // CHUNK):
                at = pl.ds(c * CHUNK, CHUNK)
                remain = refresh(at, across)
                x_ref[at, across] = remain.astype(bf16)
                norm = norm + fold(remain * remain)
            first_product(0, lx_refs[0], x_ref[:, across], across)
        norm_ref[...] = norm
        for t in range(tiles):
            lx = lx_refs[t % 2]
            if t > 0:
                first_product(t, lx, x_ref[...], slice(None))
            for h in range(halves):
                second_product(lx, h, slice(None))
                waiting.append(functools.partial(done, k * pieces + t * halves + h, t, h))
        flush()

    def put(row, value):
        rows_ref[row : row + 1, :] = jnp.sum(value, axis=0, keepdims=True)

    @pl.loop(0, MATVECS)
    def _(k):
        pl.when(k == 0)(start_from_guess)
        pl.when(k > 0)(functools.partial(continue_from, k))

        def own(c, carry):
            at = pl.ds(pl.multiple_of(c * CHUNK, CHUNK), CHUNK)
            current = x_ref[at, :].astype(f32)
            basis_ref[k, at, :] = x_ref[at, :]
            y_ref[at, :] = (current * pinv_ref[at, :]).astype(bf16)
            lifted = y_ref[at, :].astype(f32)
            new = []
            for j in range(MATVECS):
                vector = basis_ref[j, at, :].astype(f32)
                new.append(fold(vector * current))
                new.append(fold(vector * lifted))
            new.append(fold(lifted * lifted))
            return tuple(a + b for a, b in zip(carry, new))

        zero = jnp.zeros((8, 128), f32)
        mine = lax.fori_loop(0, width // CHUNK, own, (zero,) * (2 * MATVECS + 1))
        for j in range(MATVECS):
            put(2 * MATVECS + j, mine[2 * j])
            put(3 * MATVECS + j, mine[2 * j + 1])
        put(4 * MATVECS + 2, mine[2 * MATVECS])
        put(4 * MATVECS + 3, norm_ref[...])

        carry = (zero,) * (2 * MATVECS + 2)
        for piece in range(pieces):
            t, h = divmod(piece, halves)
            n = k * pieces + piece
            across = pl.ds(h * COLS, COLS)

            @pl.when(sec > 0)
            def _():
                up_copy(n).wait_recv()

            @pl.when(sec < secs - 1)
            def _():
                low_copy(n).wait_recv()

            for c in range(ROWS // BLOCK):
                inner = pl.ds(c * BLOCK, BLOCK)
                at = pl.ds(t * ROWS + c * BLOCK, BLOCK)
                image = stay_ref[at, across] + up_in[n, inner, :].astype(f32)
                image = image + low_in[n, inner, :].astype(f32)
                image_ref[at, across] = image
                lifted_half[at, across] = (image * pinv_ref[at, across]).astype(bf16)
                image_half[at, across] = image.astype(bf16)
                lifted = lifted_half[at, across].astype(f32)
                image = image_half[at, across].astype(f32)
                new = []
                for j in range(MATVECS):
                    vector = basis_ref[j, at, across].astype(f32)
                    new.append(fold(vector * image))
                    new.append(fold(vector * lifted))
                new.append(fold(lifted * lifted))
                new.append(fold(lifted * y_ref[at, across].astype(f32)))
                carry = tuple(a + b for a, b in zip(carry, new))
        for j in range(MATVECS):
            put(j, carry[2 * j])
            put(MATVECS + j, carry[2 * j + 1])
        put(4 * MATVECS, carry[2 * MATVECS])
        put(4 * MATVECS + 1, carry[2 * MATVECS + 1])

        sums = jnp.sum(rows_ref[...], axis=1, keepdims=True)
        high = sums.shape[0]
        diagonal = lax.broadcasted_iota(jnp.int32, (high, 128), 0) == lax.broadcasted_iota(
            jnp.int32, (high, 128), 1
        )
        slots_ref[k, sec] = jnp.sum(jnp.where(diagonal, sums, 0.0), axis=0, keepdims=True)
        for copy in sum_copies(k):
            copy.start()
        arrived = slots_ref.at[k, pl.ds(0, secs - 1)]
        pltpu.make_async_copy(arrived, arrived, sum_recv.at[k]).wait()
        tile = jnp.sum(slots_ref[k], axis=0) * (1.0 / count)
        tile_ref[k] = tile

        lane = lax.broadcasted_iota(jnp.int32, (1, 128), 1)

        def pick(q):
            value = jnp.sum(jnp.where(lane == q, tile, 0.0), axis=1, keepdims=True)
            return jnp.broadcast_to(value, (8, 128))

        alpha = lax.rsqrt(pick(4 * MATVECS + 3) + EPS)
        alpha_ref[k] = alpha
        theta = alpha * alpha * pick(k)
        coef_ref[0] = alpha
        coef_ref[1] = theta * alpha
        across_tile = lax.broadcasted_iota(jnp.int32, (8, 128), 1)
        down_tile = lax.broadcasted_iota(jnp.int32, (8, 128), 0)
        column = jnp.zeros((8, 128), f32)
        for j in range(MATVECS):
            other = jnp.where(k == j, alpha, alpha_ref[j])
            weight = other * alpha * (pick(MATVECS + j) - theta * pick(3 * MATVECS + j))
            inner_ref[j] = weight
            coef_ref[2 + j] = weight * other
            column = jnp.where(down_tile == j, other * alpha * pick(j), column)
        proj_ref[...] = jnp.where(across_tile == k, column, proj_ref[...])

    lane = lax.broadcasted_iota(jnp.int32, (1, 128), 1)

    def entry(i, q):
        value = jnp.sum(jnp.where(lane == q, tile_ref[i], 0.0), axis=1, keepdims=True)
        return jnp.broadcast_to(value, (8, 128))

    last = MATVECS - 1
    theta = alpha_ref[last] * alpha_ref[last] * entry(last, last)
    norm_sq = (
        entry(last, 4 * MATVECS) - 2.0 * theta * entry(last, 4 * MATVECS + 1)
        + theta * theta * entry(last, 4 * MATVECS + 2)
    )
    norm_sq = norm_sq * alpha_ref[last] * alpha_ref[last]
    for i in range(MATVECS):
        inside = coef_ref[2 + i] * alpha_ref[i] * entry(i, 2 * MATVECS + i) - 2.0 * inner_ref[i]
        for j in range(i):
            inside = inside + 2.0 * coef_ref[2 + j] * alpha_ref[i] * entry(i, 2 * MATVECS + j)
        norm_sq = norm_sq + inner_ref[i] * inside
    coef_ref[2 + MATVECS] = lax.rsqrt(jnp.maximum(norm_sq, 0.0) + EPS)

    @pl.loop(0, width // CHUNK)
    def _(c):
        at = pl.ds(pl.multiple_of(c * CHUNK, CHUNK), CHUNK)
        remain = refresh(at, slice(None))
        next_ref[at, :] = spread(coef_ref[2 + MATVECS], remain).astype(bf16)
        image_ref[at, :] = masked(spread(alpha_ref[last], image_ref[at, :]), c * CHUNK)

    projected_ref[...] = proj_ref[:MATVECS, :MATVECS]

    send_inv.wait_send()
    for copy in send_block:
        copy.wait_send()

    @pl.when(sec < secs - 1)
    def _():
        @pl.loop(0, MATVECS * pieces)
        def _(n):
            up_copy(n).wait_send()

    @pl.when(sec > 0)
    def _():
        @pl.loop(0, MATVECS * pieces)
        def _(n):
            low_copy(n).wait_send()

    @pl.loop(0, MATVECS)
    def _(r):
        sent = slots_ref.at[r, pl.ds(0, secs - 1)]
        pltpu.make_async_copy(sent, sent, sum_send.at[r]).wait()


def finish(next_in, image_in, projected_in, next_ref, image_ref, projected_ref, next_held, image_held, projected_held, into, out):
    parts, rows, _ = image_held.shape
    loads, stores = [], []
    for p in range(parts):
        at = pl.ds(p * rows, rows)
        loads.append(pltpu.make_async_copy(image_in.at[at], image_held.at[p], into.at[2 * p]))
        stores.append(pltpu.make_async_copy(image_held.at[p], image_ref.at[at], out.at[2 * p]))
        loads.append(pltpu.make_async_copy(next_in.at[at], next_held.at[p], into.at[2 * p + 1]))
        stores.append(pltpu.make_async_copy(next_held.at[p], next_ref.at[at], out.at[2 * p + 1]))
    loads.append(pltpu.make_async_copy(projected_in, projected_held, into.at[2 * parts]))
    stores.append(pltpu.make_async_copy(projected_held, projected_ref, out.at[2 * parts]))
    for copy in loads:
        copy.start()
    for arrive, leave in zip(loads, stores):
        arrive.wait()
        leave.start()
    for copy in stores:
        copy.wait()


def per_device(
    left_env, right_env, left_block, right_block, inv_sv, precond, sector_dims, channel_charge
):
    segs, secs = lax.axis_size("seg"), lax.axis_size("sec")
    channels, width = left_env.shape[2], left_env.shape[-1]
    pieces = (width // ROWS) * (width // COLS)
    halos = MATVECS * pieces
    f32, bf16 = jnp.float32, jnp.bfloat16
    vmem = pl.BlockSpec(memory_space=pltpu.VMEM)
    smem = pl.BlockSpec(memory_space=pltpu.SMEM)
    hbm = pl.BlockSpec(memory_space=pl.ANY)
    out_shape = (
        jax.ShapeDtypeStruct((width, width), bf16),
        jax.ShapeDtypeStruct((width, width), f32),
        jax.ShapeDtypeStruct((MATVECS, MATVECS), f32),
    )
    results = pl.pallas_call(
        functools.partial(kernel, segs, secs),
        name="davidson",
        out_shape=out_shape,
        in_specs=[smem, smem, hbm, hbm, hbm, hbm, vmem, hbm],
        out_specs=(vmem, vmem, vmem),
        scratch_shapes=[
            pltpu.VMEM((channels, width, width), bf16),
            pltpu.VMEM((channels, width, width), bf16),
            pltpu.VMEM((channels, width, width), bf16),
            pltpu.VMEM((channels, ROWS, width), bf16),
            pltpu.VMEM((channels, ROWS, width), bf16),
            pltpu.VMEM((width, width), bf16),
            pltpu.VMEM((width, width), f32),
            pltpu.VMEM((width // COLS, width, COLS), bf16),
            pltpu.VMEM((1, width), bf16),
            pltpu.VMEM((width, width), bf16),
            pltpu.VMEM((width, width), f32),
            pltpu.VMEM((MATVECS, width, width), bf16),
            pltpu.VMEM((channels + 1, ROWS, COLS), f32),
            pltpu.VMEM((channels + 1, ROWS, COLS), f32),
            pltpu.VMEM((3, pieces, ROWS, COLS), f32),
            pltpu.VMEM((width, width), bf16),
            pltpu.VMEM((width, width), bf16),
            pltpu.VMEM((width, width), bf16),
            pltpu.VMEM((width, width), f32),
            pltpu.VMEM((halos, ROWS, COLS), bf16),
            pltpu.VMEM((halos, ROWS, COLS), bf16),
            pltpu.VMEM((halos, ROWS, COLS), bf16),
            pltpu.VMEM((halos, ROWS, COLS), bf16),
            pltpu.VMEM((width, width), bf16),
            pltpu.VMEM((8, 128), f32),
            pltpu.VMEM((MATVECS, secs, 1, 128), f32),
            pltpu.VMEM((pl.cdiv(QUANTITIES, 8) * 8, 128), f32),
            pltpu.VMEM((MATVECS, 1, 128), f32),
            pltpu.VMEM((MATVECS, 8, 128), f32),
            pltpu.VMEM((MATVECS, 8, 128), f32),
            pltpu.VMEM((MATVECS + 3, 8, 128), f32),
            pltpu.VMEM((8, 128), f32),
            pltpu.SMEM((channels,), jnp.int32),
            pltpu.SemaphoreType.DMA((4,)),
            pltpu.SemaphoreType.DMA((1 + width // COLS,)),
            pltpu.SemaphoreType.DMA((1 + width // COLS,)),
            pltpu.SemaphoreType.DMA((2, halos)),
            pltpu.SemaphoreType.DMA((2, halos)),
            pltpu.SemaphoreType.DMA((MATVECS,)),
            pltpu.SemaphoreType.DMA((MATVECS,)),
        ],
        compiler_params=pltpu.CompilerParams(
            collective_id=0, has_side_effects=True, vmem_limit_bytes=60 * 1024 * 1024
        ),
    )(
        channel_charge, sector_dims[0, 0], left_env[0, 0], right_env[0, 0],
        left_block[0, 0], right_block[0, 0], inv_sv[0], precond[0, 0],
    )
    parts = width // ROWS
    following, image, projected = pl.pallas_call(
        finish, name="finish", out_shape=out_shape,
        in_specs=[hbm] * 3, out_specs=(hbm, hbm, hbm),
        scratch_shapes=[
            pltpu.VMEM((parts, ROWS, width), bf16),
            pltpu.VMEM((parts, ROWS, width), f32),
            pltpu.VMEM((MATVECS, MATVECS), f32),
            pltpu.SemaphoreType.DMA((2 * parts + 1,)),
            pltpu.SemaphoreType.DMA((2 * parts + 1,)),
        ],
    )(*results)
    return following[None, None], image[None, None], projected[None]


def solution(mesh):
    in_specs = (
        P("seg", "sec", None, None, None),
        P("seg", "sec", None, None, None),
        P("seg", "sec", None, None),
        P("seg", "sec", None, None),
        P("seg", "sec", None),
        P("seg", "sec", None, None),
        P("seg", "sec", None),
        P(),
    )
    out_specs = (P("seg", "sec", None, None), P("seg", "sec", None, None), P("seg", None, None))
    return jax.shard_map(
        per_device, mesh=mesh, in_specs=in_specs, out_specs=out_specs, check_vma=False
    )
```
